256 devices in a mesh: rep: 32 (over y, z), tp: 8 (over x, core).
Axes of the slice: x: 4, y: 4, z: 8, core: 2. Of those that a mesh axis runs over, the one named last changes fastest.
Arguments:
- reference_rows: bfloat16 [32768, 8192], P('rep', 'tp'), may hold values from -7 to 7
- critic_rows: bfloat16 [32768, 4096], P('rep', 'tp'), may hold values from -7 to 7
- segment_ids: int32 [32768], P('rep'), may hold values from -1 to 32767, as said below
- pack_dest: int32 [32, 32], P('rep'), may hold values from 0 to 31, as said below
- ref_query: bfloat16 [8192, 4096], P('rep', 'tp'), may hold values from -2 to 2
- ref_key: bfloat16 [8192, 1024], P('rep', 'tp'), may hold values from -2 to 2
- ref_value: bfloat16 [8192, 1024], P('rep', 'tp'), may hold values from -0.0625 to 0.0625
- critic_query: bfloat16 [4096, 4096], P(None, 'tp'), may hold values from -2 to 2
- critic_key: bfloat16 [4096, 1024], P(None, 'tp'), may hold values from -2 to 2
- critic_value: bfloat16 [4096, 1024], P(None, 'tp'), may hold values from -0.09375 to 0.09375
- ref_readout: bfloat16 [4096], P('tp'), may hold values from -0.09375 to 0.09375
- critic_readout: bfloat16 [4096], P('tp'), may hold values from -0.09375 to 0.09375
Outputs:
- ref_score: float32 [32768], P('rep')
- value: float32 [32768], P('rep')
The draws below stay inside these ranges and needn't reach their ends.
Inputs may be any that keep to these rules, and one draw needn't show every extreme that they name: Each row is a permutation: block b of replica s goes to pack pack_dest[s, b]. `segment_ids`: in every aligned block of 32 slots the used rows come first and the rest hold -1; a block holds 1 to 31 used rows, and every pack receives exactly 31 used rows from some replica and exactly 512 used rows in all. A rollout is a run of consecutive used rows with one id inside one block; different rollouts have different ids.
All inputs are finite; a program needn't handle non-finite values.
Results may differ from the reference program's by a relative error of at most 0.0084.
Values may be sent and summed in bfloat16 or wider, within the bound.
No kernel may reach another device: no remote copies, remote signals or barrier semaphores. Data moves between devices by JAX's collectives and lax.ppermute only.
A program may use at most 128 MiB of HBM per device.

```python
import jax
import jax.numpy as jnp
from jax import lax

DR = 8192
HR = 32
KR = 8
DC = 4096
HC = 32
KC = 8
HD = 128
CAP = 16
PACK = 512
TOKENS = 32768


def shared_plan(key):
    replicas = PACK // CAP
    base = jax.random.fold_in(key, 11)
    streams = jax.random.split(base, 6)
    orders = jax.vmap(lambda single: jax.random.permutation(single, replicas))(jax.random.split(streams[0], replicas)).astype(jnp.int32)
    reach = jax.random.randint(streams[1], (replicas, 1), 0, CAP)
    spread = jax.random.randint(streams[2], (replicas, replicas), 0, CAP * 64) % (reach + 1)
    leader = jax.random.randint(streams[3], (replicas,), 0, replicas)
    offsets = jax.random.randint(streams[4], (replicas,), 1, replicas)
    columns = jnp.arange(replicas)
    spread = spread.at[leader, columns].set(CAP - 1)
    spread = spread.at[(leader + offsets) % replicas, columns].set(0)
    partner = (jnp.arange(replicas)[:, None] + offsets[None, :]) % replicas
    used = CAP + spread - jnp.take_along_axis(spread, partner, axis=0)
    used_blocks = jnp.take_along_axis(used, orders, axis=1)
    starts = jax.random.randint(streams[5], (replicas, replicas, 2 * CAP), 0, 64) == 0
    starts = starts.at[:, :, 0].set(True)
    slots = jnp.arange(2 * CAP)
    live = slots[None, None, :] < used_blocks[:, :, None]
    live_starts = (starts & live).astype(jnp.int32)
    within = jnp.cumsum(live_starts, axis=-1) - 1
    count = jnp.sum(live_starts, axis=-1, keepdims=True)
    block_base = (jnp.arange(replicas)[:, None] * replicas + jnp.arange(replicas)[None, :]) * (2 * CAP)
    idents = block_base[:, :, None] + 2 * CAP - count + within
    segments = jnp.where(live, idents, -1)
    return (orders, segments.reshape(-1).astype(jnp.int32))


def draw_pack_dest(key, part):
    return shared_plan(key)[0]


def draw_segment_ids(key, part):
    return shared_plan(key)[1]


def tilted_weight(key, salt, rows_count, columns):
    base_draw = jax.random.truncated_normal(jax.random.fold_in(key, salt), -4.0, 4.0, (rows_count, columns), jnp.float32)
    result = base_draw * float(rows_count) ** (-0.5)
    return result


def drawn_rows(key, salt, width):
    result = jax.random.truncated_normal(jax.random.fold_in(key, salt), -5.0, 5.0, (TOKENS, width), jnp.float32)
    return result


def draw_reference_rows(key, part):
    return drawn_rows(key, 61, DR).astype(jnp.bfloat16)


def draw_critic_rows(key, part):
    return drawn_rows(key, 62, DC).astype(jnp.bfloat16)


def draw_ref_query(key, part):
    return tilted_weight(key, 51, DR, HR * HD).astype(jnp.bfloat16)


def draw_ref_key(key, part):
    return tilted_weight(key, 52, DR, KR * HD).astype(jnp.bfloat16)


def draw_critic_query(key, part):
    return tilted_weight(key, 53, DC, HC * HD).astype(jnp.bfloat16)


def draw_critic_key(key, part):
    return tilted_weight(key, 54, DC, KC * HD).astype(jnp.bfloat16)


def levels(key, extent, cuts, low, top_value):
    level = 1.0
    for dim, blocks in cuts:
        heights = jax.random.uniform(jax.random.fold_in(jax.random.fold_in(key, 6), dim), (blocks,), jnp.float32, low / len(cuts), top_value / len(cuts))
        level = level * jnp.repeat(jnp.exp(heights), extent[dim] // blocks).reshape((-1,) + (1,) * (len(extent) - 1 - dim))
    return level


def gaussian(rng, dims, scale, bound, cuts=(), kind=jnp.bfloat16):
    array = jax.random.normal(rng, dims, jnp.float32) * scale
    if len(cuts) > 0:
        array = levels(rng, dims, cuts, -0.22, 0.18) * array
    return jnp.clip(array, min=-bound, max=bound).astype(kind)


def setup_inputs(seed: int = 0) -> dict:
    arg_keys = jax.random.split(jax.random.key(seed), 13)
    return {
        "reference_rows": draw_reference_rows(jax.random.fold_in(arg_keys[12], 71), 0),
        "critic_rows": draw_critic_rows(jax.random.fold_in(arg_keys[12], 71), 0),
        "segment_ids": draw_segment_ids(jax.random.fold_in(arg_keys[12], 71), 0),
        "pack_dest": draw_pack_dest(jax.random.fold_in(arg_keys[12], 71), 0),
        "ref_query": draw_ref_query(jax.random.fold_in(arg_keys[12], 71), 0),
        "ref_key": draw_ref_key(jax.random.fold_in(arg_keys[12], 71), 0),
        "ref_value": gaussian(arg_keys[6], (DR, KR * HD), DR ** -0.5, 0.0625, ((0, 32), (1, 8))),
        "critic_query": draw_critic_query(jax.random.fold_in(arg_keys[12], 71), 0),
        "critic_key": draw_critic_key(jax.random.fold_in(arg_keys[12], 71), 0),
        "critic_value": gaussian(arg_keys[9], (DC, KC * HD), DC ** -0.5, 0.09375, ((1, 8),)),
        "ref_readout": gaussian(arg_keys[10], (HR * HD,), (HR * HD) ** -0.5, 0.09375, ((0, 8),)),
        "critic_readout": gaussian(arg_keys[11], (HC * HD,), (HC * HD) ** -0.5, 0.09375, ((0, 8),)),
    }


def normalize(source):
    widened = source.astype(jnp.float32)
    scale_row = lax.rsqrt(lax.optimization_barrier(jnp.mean(widened * widened, axis=-1, keepdims=True)) + 1e-05)
    return (widened * scale_row).astype(jnp.bfloat16)

def attend(queries, keys_in, values_in, segments):
    row_count = queries.shape[0]
    groups = keys_in.shape[1] // HD
    shared = queries.shape[1] // keys_in.shape[1]
    query_four = queries.astype(jnp.float32).reshape(row_count, groups, shared, HD)
    key_three = keys_in.astype(jnp.float32).reshape(row_count, groups, HD)
    value_three = values_in.astype(jnp.float32).reshape(row_count, groups, HD)
    scores = jnp.einsum('pgjd,qgd->gjpq', query_four, key_three) * HD ** (-0.5)
    position = jnp.arange(row_count)
    allowed = (position[None, :] <= position[:, None]) & (segments[:, None] == segments[None, :])
    masked = jnp.where(allowed, scores, -1e+30)
    row_max = lax.optimization_barrier(jnp.max(masked, axis=-1, keepdims=True))
    powers = jnp.where(allowed, jnp.exp(masked - row_max), 0.0)
    weights = (powers / lax.optimization_barrier(jnp.sum(powers, axis=-1, keepdims=True))).astype(jnp.bfloat16)
    mixture = jnp.einsum('gjpq,qgd->pgjd', weights.astype(jnp.float32), value_three)
    return mixture.reshape(row_count, groups * shared * HD).astype(jnp.bfloat16)

def section(rows_in, segments, w_query, w_key, w_value):
    normed = normalize(rows_in)
    queries = jnp.dot(normed, w_query, preferred_element_type=jnp.float32).astype(jnp.bfloat16)
    keys_in = jnp.dot(normed, w_key, preferred_element_type=jnp.float32).astype(jnp.bfloat16)
    values_in = jnp.dot(normed, w_value, preferred_element_type=jnp.float32).astype(jnp.bfloat16)
    return attend(queries, keys_in, values_in, segments)

def compact_index(segments):
    row_count = segments.shape[0]
    sort_keys = jnp.where(segments >= 0, 0, row_count).astype(jnp.int32) + jnp.arange(row_count, dtype=jnp.int32)
    return jnp.argsort(sort_keys)[:row_count // 2].astype(jnp.int32)

def reference(reference_rows, critic_rows, segment_ids, pack_dest, ref_query, ref_key, ref_value, critic_query, critic_key, critic_value, ref_readout, critic_readout):
    replicas = pack_dest.shape[0]
    block_rows = 2 * CAP
    inverse = jnp.argsort(pack_dest, axis=1).astype(jnp.int32)

    def to_packs(source):
        rest = source.shape[1:]
        blocks = source.reshape((replicas, replicas, block_rows) + rest)
        index_shape = (replicas, replicas) + (1,) * (1 + len(rest))
        picked = jnp.take_along_axis(blocks, inverse.reshape(index_shape), axis=1)
        return jnp.swapaxes(picked, 0, 1).reshape((replicas, replicas * block_rows) + rest)
    ref_packs = to_packs(reference_rows)
    critic_packs = to_packs(critic_rows)
    id_packs = to_packs(segment_ids)

    def one_pack(inputs):
        ref_pack, critic_pack, id_pack = inputs
        chosen = compact_index(id_pack)
        pack_ids = id_pack[chosen]
        ref_attn = section(ref_pack[chosen], pack_ids, ref_query, ref_key, ref_value)
        critic_attn = section(critic_pack[chosen], pack_ids, critic_query, critic_key, critic_value)
        ref_part = jnp.dot(ref_attn, ref_readout, preferred_element_type=jnp.float32)
        critic_part = jnp.dot(critic_attn, critic_readout, preferred_element_type=jnp.float32)
        pack_scores = jnp.stack([ref_part, critic_part])
        expanded = jnp.zeros((2, id_pack.shape[0]), jnp.float32)
        return expanded.at[:, chosen].set(pack_scores)
    results = lax.map(one_pack, (ref_packs, critic_packs, id_packs))
    returned = results.reshape(replicas, 2, replicas, block_rows).transpose(2, 1, 0, 3)
    ordered = jnp.take_along_axis(returned, pack_dest.reshape(replicas, 1, replicas, 1), axis=2)
    used = segment_ids.reshape(replicas, 1, replicas, block_rows) >= 0
    ordered = jnp.where(used, ordered, 0.0)
    return (ordered[:, 0].reshape(-1), ordered[:, 1].reshape(-1))
```

```python
import functools

import jax
import jax.numpy as jnp
from jax import lax
from jax.experimental import pallas as pl
from jax.experimental.pallas import tpu as pltpu
from jax.sharding import PartitionSpec as P

HD = 128
NY, NZ, NX = 4, 8, 4
WIDE = 768
EPS = 1e-05
BF = jnp.bfloat16
F32 = jnp.float32


def shift_x(v, k):
    pairs = [(2 * x + c, 2 * ((x + k) % NX) + c) for x in range(NX) for c in range(2)]
    return lax.ppermute(v, "tp", pairs)


def swap_core(v):
    return lax.ppermute(v, "tp", [(t, t ^ 1) for t in range(2 * NX)])


def shift_rep(v, dy, dz):
    pairs = [
        (y * NZ + z, ((y + dy) % NY) * NZ + (z + dz) % NZ) for y in range(NY) for z in range(NZ)
    ]
    return lax.ppermute(v, "rep", pairs)


def around(v, shift):
    half = v.shape[0] // 2
    before = shift(v, 1)
    after = shift(v, -1)
    opposite_a = shift(before[:half], 1)
    opposite_b = shift(after[half:], -1)
    return v, after, opposite_a, opposite_b, before


def weights_over_rep(v):
    own, after, opp_a, opp_b, before = around(v, lambda a, k: shift_rep(a, k, 0))
    mine = jnp.stack([own, after, jnp.concatenate([opp_a, opp_b]), before])
    pieces = [(0, 0, mine)]
    low = high = mine
    for step in range(1, 4):
        low = shift_rep(low, 0, 1)
        high = shift_rep(high, 0, -1)
        pieces += [(-step, 0, low), (step, 0, high)]
    pieces += [(4, 0, shift_rep(low[:2], 0, 1)), (4, 2, shift_rep(high[2:], 0, -1))]
    return pieces


def project_kernel(plan_x, plan_keep, plan_send, n_x, n_w, k_rows, *refs):
    pos = refs[0]
    xs = refs[1 : 1 + n_x]
    ws = refs[1 + n_x : 1 + n_x + n_w]
    keep_ref, send_ref, xbuf, wbuf, sems = refs[1 + n_x + n_w :]
    copies = {"x": [], "keep": [], "send": []}
    for slot, (kind, plan, sources, dst) in enumerate(
        (
            ("x", plan_x, xs, xbuf),
            ("keep", plan_keep, ws, wbuf),
            ("send", plan_send, ws, wbuf),
        )
    ):
        for which, place in plan:
            src, at = place(pos, sources[which])
            copies[kind].append(pltpu.make_async_copy(src, dst.at[at], sems.at[slot]))
    for kind in ("x", "keep", "send"):
        for copy in copies[kind]:
            copy.start()
    rows = xbuf.shape[0]

    def wait(kind):
        for copy in copies[kind]:
            copy.wait()

    wait("x")
    squares = jnp.zeros((rows, 128), F32)

    def add_square(k, total):
        part = xbuf[:, pl.ds(pl.multiple_of(k * 128, 128), 128)].astype(F32)
        return total + part * part

    squares = lax.fori_loop(0, k_rows // 128, add_square, squares)
    keep_ref[:, WIDE:] = squares
    send_ref[:, WIDE:] = squares
    wait("keep")
    for base, out in ((0, keep_ref), (WIDE, send_ref)):
        if base:
            wait("send")

        @pl.loop(0, WIDE // 256)
        def _(n):
            src = pl.ds(pl.multiple_of(base + n * 256, 256), 256)
            dst = pl.ds(pl.multiple_of(n * 256, 256), 256)
            out[:, dst] = jnp.dot(xbuf[...], wbuf[:, src], preferred_element_type=F32)


def project(pos, xs, ws, plan_x, plan_keep, plan_send, rows, k_rows):
    hbm = pl.BlockSpec(memory_space=pl.ANY)
    vmem = pl.BlockSpec(memory_space=pltpu.VMEM)
    out = jax.ShapeDtypeStruct((rows, WIDE + 128), F32)
    return pl.pallas_call(
        functools.partial(
            project_kernel, plan_x, plan_keep, plan_send, len(xs), len(ws), k_rows
        ),
        out_shape=(out, out),
        in_specs=[pl.BlockSpec(memory_space=pltpu.SMEM)] + [hbm] * (len(xs) + len(ws)),
        out_specs=(vmem, vmem),
        scratch_shapes=[
            pltpu.VMEM((rows, k_rows), BF),
            pltpu.VMEM((k_rows, 2 * WIDE), BF),
            pltpu.SemaphoreType.DMA((3,)),
        ],
        compiler_params=pltpu.CompilerParams(vmem_limit_bytes=48 * 1024 * 1024),
        cost_estimate=pl.CostEstimate(
            flops=2 * rows * k_rows * 2 * WIDE,
            bytes_accessed=2 * k_rows * (rows + 2 * WIDE) + 8 * rows * (WIDE + 128),
            transcendentals=0,
        ),
    )(pos, *xs, *ws)


def attend_kernel(depth, keep_ref, recv_ref, seg_row, seg_col, read_ref, out_ref):
    both = keep_ref[...] + recv_ref[...]
    mean = jnp.sum(both[:, WIDE:], axis=-1, keepdims=True) * (1.0 / depth)
    rows = (both[:, :WIDE] * lax.rsqrt(mean + EPS)).astype(BF)
    tile = rows.shape[0]
    queries = jnp.concatenate([rows[:, h * HD : (h + 1) * HD] for h in range(4)], axis=0)
    keys, values = rows[:, 4 * HD : 5 * HD], rows[:, 5 * HD :]
    scores = (
        lax.dot_general(queries, keys, (((1,), (1,)), ((), ())), preferred_element_type=F32)
        * HD ** (-0.5)
    )
    ids = lax.broadcasted_iota(jnp.int32, (tile, tile), 0)
    jds = lax.broadcasted_iota(jnp.int32, (tile, tile), 1)
    allowed = (jds <= ids) & (seg_col[...] == seg_row[...])
    bias = jnp.where(allowed, 0.0, -1e30)
    bias = jnp.concatenate([bias] * 4, axis=0)
    masked = jnp.where(bias < 0.0, -1e30, scores)
    powers = jnp.exp(masked - jnp.max(masked, axis=-1, keepdims=True))
    weights = (powers / jnp.sum(powers, axis=-1, keepdims=True)).astype(BF)
    mixture = jnp.dot(weights, values, preferred_element_type=F32).astype(BF)
    total = jnp.zeros((8, tile), F32)
    for h in range(4):
        total += lax.dot_general(
            read_ref[h],
            mixture[h * tile : (h + 1) * tile],
            (((1,), (1,)), ((), ())),
            preferred_element_type=F32,
        )
    out_ref[...] = total


def attend(keep, recv, seg_row, seg_col, readout, depth):
    rows = keep.shape[0]
    tile = 128
    read = jnp.broadcast_to(readout.reshape(4, 1, HD), (4, 8, HD))
    wide = pl.BlockSpec((tile, WIDE + 128), lambda i: (i, 0))
    return pl.pallas_call(
        functools.partial(attend_kernel, depth),
        grid=(rows // tile,),
        out_shape=jax.ShapeDtypeStruct((8, rows), F32),
        in_specs=[
            wide,
            wide,
            pl.BlockSpec((1, tile), lambda i: (0, i)),
            pl.BlockSpec((tile, 1), lambda i: (i, 0)),
            pl.BlockSpec((4, 8, HD), lambda i: (0, 0, 0)),
        ],
        out_specs=pl.BlockSpec((8, tile), lambda i: (0, i)),
        cost_estimate=pl.CostEstimate(
            flops=rows * 4 * tile * HD * 4,
            bytes_accessed=rows * (WIDE + 128) * 8,
            transcendentals=rows * 4 * tile,
        ),
    )(keep, recv, seg_row, seg_col, read)


def aligned(value, step):
    return pl.multiple_of(value, step)


def x_plan(rows, width, lanes):
    plan = []
    half = rows // 2
    for which, ahead, first, count in (
        (0, 0, 0, rows),
        (1, 1, 0, rows),
        (2, 2, 0, half),
        (3, 2, half, half),
        (4, 3, 0, rows),
    ):
        for lane, size, offset in lanes:

            def place(pos, src, ahead=ahead, first=first, count=count, lane=lane, size=size, offset=offset):
                origin = lax.rem(pos[0] + ahead, NX)
                at = aligned(origin * width + offset(pos[1]), 128)
                return src.at[:, pl.ds(lane, size)], (pl.ds(first, count), pl.ds(at, size))

            plan.append((which, place))
    return plan


def body(
    reference_rows,
    critic_rows,
    segment_ids,
    pack_dest,
    ref_query,
    ref_key,
    ref_value,
    critic_query,
    critic_key,
    critic_value,
    ref_readout,
    critic_readout,
):
    del pack_dest
    rep, tp = lax.axis_index("rep"), lax.axis_index("tp")
    x, core = tp // 2, tp % 2
    y, z = rep // NZ, rep % NZ
    pos = jnp.stack([x, core, y, z]).astype(jnp.int32)
    first = core == 0

    ref_w = jnp.concatenate([ref_query, ref_key, ref_value], axis=1)
    upper, lower = ref_w[:128], ref_w[128:]
    ref_keep = jnp.where(first, upper, lower)
    ref_send = swap_core(jnp.where(first, lower, upper))
    keep_all = lax.all_gather(ref_keep, "rep", axis=0, tiled=True)
    send_pieces = weights_over_rep(ref_send)

    critic_w = [w.reshape(NX, 2, 512, -1) for w in (critic_query, critic_key, critic_value)]
    critic_send = swap_core(
        jnp.concatenate(
            [lax.dynamic_index_in_dim(w, 1 - core, 1, keepdims=False) for w in critic_w], axis=-1
        )
    )

    critic_shards = around(critic_rows, shift_x)

    low = jnp.concatenate([reference_rows[:, k : k + 128] for k in range(0, 1024, 256)], axis=1)
    high = jnp.concatenate([reference_rows[:, k : k + 128] for k in range(128, 1024, 256)], axis=1)
    ref_mine = jnp.where(first, low, high)
    ref_other = swap_core(jnp.where(first, high, low))
    ref_rows = jnp.concatenate([ref_mine, ref_other], axis=1)

    chunk = 512
    ref_shards = [
        around(ref_rows[start : start + chunk], shift_x) for start in range(0, 1024, chunk)
    ]

    seg_row = segment_ids.reshape(1, -1)
    seg_col = segment_ids.reshape(-1, 1)

    def critic_keep_place(lane, size):
        def make(k):
            def place(pos, src):
                return (
                    src.at[pl.ds(aligned((2 * k + pos[1]) * 512, 512), 512), :],
                    (pl.ds(k * 512, 512), pl.ds(lane, size)),
                )

            return place

        return [make(k) for k in range(NX)]

    plan_keep = [
        (i, place)
        for i, (lane, size) in enumerate(((0, 512), (512, 128), (640, 128)))
        for place in critic_keep_place(lane, size)
    ]

    def critic_send_place(k):
        def place(pos, src):
            return src.at[k], (pl.ds(k * 512, 512), pl.ds(WIDE, WIDE))

        return place

    plan_send = [(3, critic_send_place(k)) for k in range(NX)]
    keep, send = project(
        pos,
        list(critic_shards),
        [critic_query, critic_key, critic_value, critic_send],
        x_plan(1024, 512, [(0, 512, lambda c: 0)]),
        plan_keep,
        plan_send,
        1024,
        2048,
    )
    critic_part = attend(keep, swap_core(send), seg_row, seg_col, critic_readout, 4096)[:1]

    def ref_keep_place(k):
        def place(pos, src):
            return src.at[pl.ds(k * 1024, 1024), :], (pl.ds(k * 1024, 1024), pl.ds(0, WIDE))

        return place

    plan_keep = [(0, ref_keep_place(k)) for k in range(NX)]
    plan_send = []
    for index, (dz, dy0, piece) in enumerate(send_pieces):
        for j in range(piece.shape[0]):

            def place(pos, src, dz=dz, dy=dy0 + j, j=j):
                origin = lax.rem(pos[2] + dy, NY) * NZ + lax.rem(pos[3] + dz + NZ, NZ)
                return src.at[j], (pl.ds(aligned(origin * 128, 128), 128), pl.ds(WIDE, WIDE))

            plan_send.append((1 + index, place))
    ref_ws = [keep_all] + [piece for _, _, piece in send_pieces]
    lanes = [(0, 512, lambda c: c * 512), (512, 512, lambda c: (1 - c) * 512)]
    ref_parts = []
    for index, shards in enumerate(ref_shards):
        start = index * chunk
        keep, send = project(
            pos,
            list(shards),
            ref_ws,
            x_plan(chunk, 1024, lanes),
            plan_keep,
            plan_send,
            chunk,
            4096,
        )
        ref_parts.append(
            attend(
                keep,
                swap_core(send),
                seg_row[:, start : start + chunk],
                seg_col[start : start + chunk],
                ref_readout,
                8192,
            )[:1]
        )
    partial = jnp.concatenate([jnp.concatenate(ref_parts, axis=1), critic_part], axis=0)
    scores = lax.psum(partial, "tp")
    scores = jnp.where(seg_row >= 0, scores, 0.0)
    return scores[0], scores[1]


def solution(mesh):
    return jax.shard_map(
        body,
        mesh=mesh,
        in_specs=(
            P("rep", "tp"),
            P("rep", "tp"),
            P("rep"),
            P("rep", None),
            P("rep", "tp"),
            P("rep", "tp"),
            P("rep", "tp"),
            P(None, "tp"),
            P(None, "tp"),
            P(None, "tp"),
            P("tp"),
            P("tp"),
        ),
        out_specs=(P("rep"), P("rep")),
        check_vma=False,
    )
```

```python
import functools

import jax
import jax.numpy as jnp
from jax import lax
from jax.experimental import pallas as pl
from jax.experimental.pallas import tpu as pltpu
from jax.sharding import PartitionSpec as P

HD = 128
NX = 4
WIDE = 768
EPS = 1e-05
BF = jnp.bfloat16
F32 = jnp.float32
EVERY = slice(None)


def shift_x(v, k):
    pairs = [(2 * x + c, 2 * ((x + k) % NX) + c) for x in range(NX) for c in range(2)]
    return lax.ppermute(v, "tp", pairs)


def swap_core(v):
    return lax.ppermute(v, "tp", [(t, t ^ 1) for t in range(2 * NX)])


def over_tp(v):
    v = v + swap_core(v)
    return v + shift_x(v, 1) + (shift_x(v, 2) + shift_x(v, 3))


def step_one(v):
    return shift_x(v, 1), shift_x(v, -1)


def step_two(before, after):
    half = before.shape[0] // 2
    return shift_x(before[:half], 1), shift_x(after[half:], -1)


def aligned(value, step):
    return pl.multiple_of(value, step)


def cheap():
    return pl.CostEstimate(flops=1024, bytes_accessed=1024, transcendentals=0)


def attend_tiles(acc, squares, depth, seg_ref, read_ref, more_ref, out_ref):
    tile = 128
    jds = lax.broadcasted_iota(jnp.int32, (tile, tile), 0)
    ids = lax.broadcasted_iota(jnp.int32, (tile, tile), 1)

    @pl.loop(0, acc.shape[0] // tile // 2)
    def _(pair):
        for u in range(2):
            at = pl.ds(aligned((pair * 2 + u) * tile, tile), tile)
            part = acc[at, :].astype(BF)
            queries = jnp.concatenate([part[:, h * HD : (h + 1) * HD] for h in range(4)], axis=0)
            keys, values = part[:, 4 * HD : 5 * HD], part[:, 5 * HD :]
            segs = jnp.broadcast_to(seg_ref[:, at], (tile, tile))
            allowed = (jds <= ids) & (segs.T == segs)
            mean = jnp.sum(squares[at, :], axis=-1, keepdims=True) * (1.0 / depth)
            key_scale = jnp.broadcast_to(lax.rsqrt(mean + EPS), (tile, tile))
            both = key_scale * key_scale.T * HD ** (-0.5)
            scores = lax.dot_general(
                keys, queries, (((1,), (1,)), ((), ())), preferred_element_type=F32
            )
            hidden = jnp.concatenate([jnp.where(allowed, 0.0, -1e30)] * 4, axis=1) < 0.0
            masked = jnp.where(hidden, -1e30, scores * jnp.concatenate([both] * 4, axis=1))
            powers = jnp.exp(masked - jnp.max(masked, axis=0, keepdims=True))
            inverse = 1.0 / jnp.sum(powers, axis=0, keepdims=True)
            weights = (powers * inverse * jnp.concatenate([key_scale] * 4, axis=1)).astype(BF)
            mixture = lax.dot_general(
                values, weights, (((0,), (0,)), ((), ())), preferred_element_type=F32
            ).astype(BF)
            total = jnp.zeros((8, tile), F32)
            for h in range(4):
                total += jnp.dot(
                    read_ref[h], mixture[:, h * tile : (h + 1) * tile], preferred_element_type=F32
                )
            if more_ref is not None:
                total += more_ref[:, at]
            out_ref[:, at] = total


def start_copies(pos, src, dst, sem, place):
    condition, copies = place(pos)

    def start():
        for from_, to in copies:
            pltpu.make_async_copy(src.at[from_], dst.at[to], sem).start()

    if condition is None:
        start()
    else:
        pl.when(condition)(start)


def project_kernel(plan_x, plan_w, n_x, n_w, prior, finish, *refs):
    pos, refs = refs[0], refs[1:]
    xs, ws, refs = refs[:n_x], refs[n_x : n_x + n_w], refs[n_x + n_w :]
    if prior:
        prior_squares, refs = refs[0], refs[1:]
    if finish:
        seg_ref, read_ref, refs = refs[0], refs[1], refs[2:]
        more_ref, refs = (refs[0], refs[1:]) if finish[1] else (None, refs)
        out_ref, xbuf, wbuf, sems, acc, squares = refs
    else:
        acc, squares, xbuf, wbuf, sems = refs
    slots, rows, width = xbuf.shape
    for slot in range(slots):
        for plan, sources, dst, kind in ((plan_x, xs, xbuf, 0), (plan_w, ws, wbuf, 1)):
            for which, place in plan[slot]:
                start_copies(pos, sources[which], dst.at[slot], sems.at[kind, slot], place)
    acc[...] = jnp.zeros(acc.shape, F32)
    squares[...] = prior_squares[...] if prior else jnp.zeros(squares.shape, F32)

    @pl.loop(0, slots)
    def _(s):
        pltpu.make_async_copy(xbuf.at[s], xbuf.at[s], sems.at[0, s]).wait()

        @pl.when((s == 2) | (not prior))
        def _():
            @pl.loop(0, rows // 64)
            def _(m):
                at = pl.ds(aligned(m * 64, 64), 64)
                total = squares[at, :]
                for k in range(0, width, 128):
                    part = xbuf[s, at, k : k + 128].astype(F32)
                    total += part * part
                squares[at, :] = total

        pltpu.make_async_copy(wbuf.at[s], wbuf.at[s], sems.at[1, s]).wait()

        @pl.loop(0, rows // 512)
        def _(m):
            at = pl.ds(aligned(m * 512, 512), 512)
            for k in range(0, width, 1024):
                acc[at, :] += jnp.dot(
                    xbuf[s, at, k : k + 1024], wbuf[s, k : k + 1024, :], preferred_element_type=F32
                )

    if finish:
        attend_tiles(acc, squares, finish[0], seg_ref, read_ref, more_ref, out_ref)


def project(pos, xs, ws, plan_x, plan_w, width, rows, prior=(), finish=None):
    slots = len(plan_x)
    vmem = pl.BlockSpec(memory_space=pltpu.VMEM)
    operands = [pos] + [
        pltpu.with_memory_space_constraint(v, pltpu.MemorySpace.HBM) for v in (*xs, *ws)
    ]
    specs = [pl.BlockSpec(memory_space=pltpu.SMEM)]
    specs += [pl.BlockSpec(memory_space=pltpu.MemorySpace.HBM)] * (len(xs) + len(ws))
    operands += prior
    specs += [vmem] * len(prior)
    scratch = [
        pltpu.VMEM((slots, rows, width), BF),
        pltpu.VMEM((slots, width, WIDE), BF),
        pltpu.SemaphoreType.DMA((2, slots)),
    ]
    out = (jax.ShapeDtypeStruct((rows, WIDE), F32), jax.ShapeDtypeStruct((rows, 128), F32))
    static = None
    if finish:
        index, depth, segments, readout, more = finish
        at_row = (jnp.arange(8) == index)[None, :, None]
        read = jnp.where(at_row, readout.reshape(4, 1, HD), jnp.zeros((), BF))
        extra = [segments, read] + ([more] if more is not None else [])
        operands += extra
        specs += [vmem] * len(extra)
        scratch += [pltpu.VMEM((rows, WIDE), F32), pltpu.VMEM((rows, 128), F32)]
        out = jax.ShapeDtypeStruct((8, rows), F32)
        static = (depth, more is not None)
    return pl.pallas_call(
        functools.partial(
            project_kernel, plan_x, plan_w, len(xs), len(ws), len(prior) > 0, static
        ),
        out_shape=out,
        in_specs=specs,
        out_specs=vmem if finish else (vmem, vmem),
        scratch_shapes=scratch,
        compiler_params=pltpu.CompilerParams(vmem_limit_bytes=48 * 1024 * 1024),
        cost_estimate=cheap(),
    )(*operands)


def origin(pos, ahead):
    return lax.rem(pos[0] + ahead, NX)


def side(pos, other):
    return 1 - pos[1] if other else pos[1]


def critic_rows_plan(which, other, rows):
    def place(pos):
        to = (pl.ds(*rows), pl.ds(aligned(side(pos, other) * 512, 512), 512))
        return None, [((EVERY, EVERY), to)]

    return [(which, place)]


def critic_weights(ahead):
    plan = []
    for which, (lane, size) in enumerate(((0, 512), (512, 128), (640, 128))):

        def place(pos, lane=lane, size=size):
            rows = pl.ds(aligned(origin(pos, ahead) * 1024, 1024), 1024)
            return None, [((rows, EVERY), (EVERY, pl.ds(lane, size)))]

        plan.append((which, place))
    return plan


def ref_rows_plan(which, other, rows):
    def place(pos):
        to = (pl.ds(*rows), pl.ds(aligned(side(pos, other) * 1024, 1024), 1024))
        return None, [((EVERY, EVERY), to)]

    return [(which, place)]


def gathered_weights(which, ahead):
    def place(pos):
        rows = pl.ds(aligned(origin(pos, ahead) * 2048, 2048), 2048)
        return None, [((rows, EVERY), (EVERY, EVERY))]

    return [(which, place)]


def squares_kernel(*refs):
    xs, out_ref = refs[:-1], refs[-1]

    @pl.loop(0, out_ref.shape[0] // 64)
    def _(m):
        at = pl.ds(aligned(m * 64, 64), 64)
        total = jnp.zeros((64, 128), F32)
        for block in xs:
            for k in range(0, block.shape[1], 128):
                part = block[at, k : k + 128].astype(F32)
                total += part * part
        out_ref[at, :] = total


def squares(xs):
    rows, tile = xs[0].shape[0], 256
    return pl.pallas_call(
        squares_kernel,
        grid=(rows // tile,),
        out_shape=jax.ShapeDtypeStruct((rows, 128), F32),
        in_specs=[pl.BlockSpec((tile, v.shape[1]), lambda i: (i, 0)) for v in xs],
        out_specs=pl.BlockSpec((tile, 128), lambda i: (i, 0)),
        cost_estimate=cheap(),
    )(*[pltpu.with_memory_space_constraint(v, pltpu.MemorySpace.HBM) for v in xs])


def body(
    reference_rows,
    critic_rows,
    segment_ids,
    pack_dest,
    ref_query,
    ref_key,
    ref_value,
    critic_query,
    critic_key,
    critic_value,
    ref_readout,
    critic_readout,
):
    del pack_dest
    tp = lax.axis_index("tp")
    pos = jnp.stack([tp // 2, tp % 2]).astype(jnp.int32)
    seg_row = segment_ids.reshape(1, -1)
    slots = segment_ids.shape[0]
    half = slots // 2

    ref_w = jnp.concatenate([ref_query, ref_key, ref_value], axis=1)
    gathered = lax.all_gather(ref_w, "rep", axis=0, tiled=True)
    critic_before, critic_after = step_one(critic_rows)
    critic_other, ref_other = swap_core(critic_rows), swap_core(reference_rows)

    critic_before, critic_after, critic_other, ref_rows, ref_other = lax.optimization_barrier(
        (critic_before, critic_after, critic_other, reference_rows, ref_other)
    )
    critic_far = step_two(critic_before, critic_after)
    critic_far, ref_rows = lax.optimization_barrier((critic_far, ref_rows))
    ref_before, ref_after = step_one(ref_rows)
    critic_x = [critic_rows, critic_other]
    for v in (critic_after, critic_before, *critic_far):
        critic_x += [v, swap_core(v)]
    plan_x = [[], [], [], []]
    order = ((0, (0, slots)), (1, (0, slots)), (3, (0, slots)), (2, (0, half)), (2, (half, half)))
    for index, (slot, rows) in enumerate(order):
        for other in range(2):
            plan_x[slot] += critic_rows_plan(2 * index + other, other == 1, rows)
    critic_part = project(
        pos,
        critic_x,
        [critic_query, critic_key, critic_value],
        plan_x,
        [critic_weights(k) for k in range(NX)],
        1024,
        slots,
        finish=(1, 4096, seg_row, critic_readout, None),
    )

    ref_before, ref_after, critic_part = lax.optimization_barrier(
        (ref_before, ref_after, critic_part)
    )
    far = step_two(ref_before, ref_after)
    ref_x = [ref_rows, ref_other]
    for v in (ref_after, ref_before):
        ref_x += [v, swap_core(v)]
    total = squares(ref_x)
    far, total = lax.optimization_barrier((far, total))
    for v in far:
        ref_x += [v, swap_core(v)]
    plan_x = [[], [], [], []]
    for index, (slot, rows) in enumerate(order):
        for other in range(2):
            plan_x[slot] += ref_rows_plan(2 * index + other, other == 1, rows)
    partial = project(
        pos,
        ref_x,
        [gathered],
        plan_x,
        [gathered_weights(0, k) for k in range(NX)],
        2048,
        slots,
        prior=(total,),
        finish=(0, 8192, seg_row, ref_readout, critic_part),
    )
    scores = over_tp(partial)
    scores = jnp.where(seg_row >= 0, scores, 0.0)
    return scores[0], scores[1]


def solution(mesh):
    return jax.shard_map(
        body,
        mesh=mesh,
        in_specs=(
            P("rep", "tp"),
            P("rep", "tp"),
            P("rep"),
            P("rep", None),
            P("rep", "tp"),
            P("rep", "tp"),
            P("rep", "tp"),
            P(None, "tp"),
            P(None, "tp"),
            P(None, "tp"),
            P("tp"),
            P("tp"),
        ),
        out_specs=(P("rep"), P("rep")),
        check_vma=False,
    )
```

```python
import functools

import jax
import jax.numpy as jnp
from jax import lax
from jax.experimental import pallas as pl
from jax.experimental.pallas import tpu as pltpu
from jax.sharding import PartitionSpec as P

HD = 128
NX = 4
WIDE = 768
EPS = 1e-05
BF = jnp.bfloat16
F32 = jnp.float32
EVERY = slice(None)


def shift_x(v, k):
    pairs = [(2 * x + c, 2 * ((x + k) % NX) + c) for x in range(NX) for c in range(2)]
    return lax.ppermute(v, "tp", pairs)


def swap_core(v):
    return lax.ppermute(v, "tp", [(t, t ^ 1) for t in range(2 * NX)])


def over_tp(v):
    v = v + swap_core(v)
    return v + shift_x(v, 1) + (shift_x(v, 2) + shift_x(v, 3))


def step_one(v):
    return shift_x(v, 1), shift_x(v, -1)


def step_two(before, after):
    half = before.shape[0] // 2
    return shift_x(before[:half], 1), shift_x(after[half:], -1)


def aligned(value, step):
    return pl.multiple_of(value, step)


def cheap():
    return pl.CostEstimate(flops=1024, bytes_accessed=1024, transcendentals=0)


def attend_tiles(acc, squares, depth, seg_ref, read_ref, more_ref, out_ref):
    tile = 128
    jds = lax.broadcasted_iota(jnp.int32, (tile, tile), 0)
    ids = lax.broadcasted_iota(jnp.int32, (tile, tile), 1)

    @pl.loop(0, acc.shape[0] // tile // 2)
    def _(pair):
        for u in range(2):
            at = pl.ds(aligned((pair * 2 + u) * tile, tile), tile)
            part = acc[at, :].astype(BF)
            queries = jnp.concatenate([part[:, h * HD : (h + 1) * HD] for h in range(4)], axis=0)
            keys, values = part[:, 4 * HD : 5 * HD], part[:, 5 * HD :]
            segs = jnp.broadcast_to(seg_ref[:, at], (tile, tile))
            allowed = (jds <= ids) & (segs.T == segs)
            mean = jnp.sum(squares[at, :], axis=-1, keepdims=True) * (1.0 / depth)
            key_scale = jnp.broadcast_to(lax.rsqrt(mean + EPS), (tile, tile))
            both = key_scale * key_scale.T * HD ** (-0.5)
            scores = lax.dot_general(
                keys, queries, (((1,), (1,)), ((), ())), preferred_element_type=F32
            )
            hidden = jnp.concatenate([jnp.where(allowed, 0.0, -1e30)] * 4, axis=1) < 0.0
            masked = jnp.where(hidden, -1e30, scores * jnp.concatenate([both] * 4, axis=1))
            powers = jnp.exp(masked - jnp.max(masked, axis=0, keepdims=True))
            inverse = 1.0 / jnp.sum(powers, axis=0, keepdims=True)
            weights = (powers * inverse * jnp.concatenate([key_scale] * 4, axis=1)).astype(BF)
            mixture = lax.dot_general(
                values, weights, (((0,), (0,)), ((), ())), preferred_element_type=F32
            ).astype(BF)
            total = jnp.zeros((8, tile), F32)
            for h in range(4):
                total += jnp.dot(
                    read_ref[h], mixture[:, h * tile : (h + 1) * tile], preferred_element_type=F32
                )
            if more_ref is not None:
                total += more_ref[:, at]
            out_ref[:, at] = total


def start_copies(pos, src, dst, sem, place):
    condition, copies = place(pos)

    def start():
        for from_, to in copies:
            pltpu.make_async_copy(src.at[from_], dst.at[to], sem).start()

    if condition is None:
        start()
    else:
        pl.when(condition)(start)


def project_kernel(plan_x, plan_w, n_x, n_w, prior, finish, *refs):
    pos, refs = refs[0], refs[1:]
    xs, ws, refs = refs[:n_x], refs[n_x : n_x + n_w], refs[n_x + n_w :]
    if prior:
        prior_squares, refs = refs[0], refs[1:]
    prior_ref, refs = (refs[0], refs[1:]) if prior > 1 else (None, refs)
    if finish:
        seg_ref, read_ref, refs = refs[0], refs[1], refs[2:]
        more_ref, refs = (refs[0], refs[1:]) if finish[1] else (None, refs)
        out_ref, xbuf, wbuf, sems, acc, squares = refs
    else:
        acc, xbuf, wbuf, sems = refs
        squares = None
    slots, rows, width = xbuf.shape
    for slot in range(slots):
        for plan, sources, dst, kind in ((plan_x, xs, xbuf, 0), (plan_w, ws, wbuf, 1)):
            for which, place in plan[slot]:
                start_copies(pos, sources[which], dst.at[slot], sems.at[kind, slot], place)
    acc[...] = prior_ref[...] if prior > 1 else jnp.zeros(acc.shape, F32)
    if finish:
        squares[...] = prior_squares[...] if prior else jnp.zeros(squares.shape, F32)

    @pl.loop(0, slots)
    def _(s):
        pltpu.make_async_copy(xbuf.at[s], xbuf.at[s], sems.at[0, s]).wait()

        if finish:

            @pl.loop(0, rows // 64)
            def _(m):
                at = pl.ds(aligned(m * 64, 64), 64)
                total = squares[at, :]
                for k in range(0, width, 128):
                    part = xbuf[s, at, k : k + 128].astype(F32)
                    total += part * part
                squares[at, :] = total

        pltpu.make_async_copy(wbuf.at[s], wbuf.at[s], sems.at[1, s]).wait()

        @pl.loop(0, rows // 512)
        def _(m):
            at = pl.ds(aligned(m * 512, 512), 512)
            for k in range(0, width, 1024):
                acc[at, :] += jnp.dot(
                    xbuf[s, at, k : k + 1024], wbuf[s, k : k + 1024, :], preferred_element_type=F32
                )

    if finish:
        attend_tiles(acc, squares, finish[0], seg_ref, read_ref, more_ref, out_ref)


def project(pos, xs, ws, plan_x, plan_w, width, rows, prior=(), finish=None):
    slots = len(plan_x)
    vmem = pl.BlockSpec(memory_space=pltpu.VMEM)
    operands = [pos] + [
        pltpu.with_memory_space_constraint(v, pltpu.MemorySpace.HBM) for v in (*xs, *ws)
    ]
    specs = [pl.BlockSpec(memory_space=pltpu.SMEM)]
    specs += [pl.BlockSpec(memory_space=pltpu.MemorySpace.HBM)] * (len(xs) + len(ws))
    operands += prior
    specs += [vmem] * len(prior)
    scratch = [
        pltpu.VMEM((slots, rows, width), BF),
        pltpu.VMEM((slots, width, WIDE), BF),
        pltpu.SemaphoreType.DMA((2, slots)),
    ]
    out = jax.ShapeDtypeStruct((rows, WIDE), F32)
    static = None
    if finish:
        index, depth, segments, readout, more = finish
        at_row = (jnp.arange(8) == index)[None, :, None]
        read = jnp.where(at_row, readout.reshape(4, 1, HD), jnp.zeros((), BF))
        extra = [segments, read] + ([more] if more is not None else [])
        operands += extra
        specs += [vmem] * len(extra)
        scratch += [pltpu.VMEM((rows, WIDE), F32), pltpu.VMEM((rows, 128), F32)]
        out = jax.ShapeDtypeStruct((8, rows), F32)
        static = (depth, more is not None)
    return pl.pallas_call(
        functools.partial(
            project_kernel, plan_x, plan_w, len(xs), len(ws), len(prior), static
        ),
        out_shape=out,
        in_specs=specs,
        out_specs=vmem,
        scratch_shapes=scratch,
        compiler_params=pltpu.CompilerParams(vmem_limit_bytes=48 * 1024 * 1024),
        cost_estimate=cheap(),
    )(*operands)


def origin(pos, ahead):
    return lax.rem(pos[0] + ahead, NX)


def side(pos, other):
    return 1 - pos[1] if other else pos[1]


def critic_rows_plan(which, other, rows):
    def place(pos):
        to = (pl.ds(*rows), pl.ds(aligned(side(pos, other) * 512, 512), 512))
        return None, [((EVERY, EVERY), to)]

    return [(which, place)]


def critic_weights(ahead):
    plan = []
    for which, (lane, size) in enumerate(((0, 512), (512, 128), (640, 128))):

        def place(pos, lane=lane, size=size):
            rows = pl.ds(aligned(origin(pos, ahead) * 1024, 1024), 1024)
            return None, [((rows, EVERY), (EVERY, pl.ds(lane, size)))]

        plan.append((which, place))
    return plan


def ref_rows_plan(which, other, rows):
    def place(pos):
        to = (pl.ds(*rows), pl.ds(aligned(side(pos, other) * 1024, 1024), 1024))
        return None, [((EVERY, EVERY), to)]

    return [(which, place)]


def gathered_weights(which, ahead):
    def place(pos):
        rows = pl.ds(aligned(origin(pos, ahead) * 2048, 2048), 2048)
        return None, [((rows, EVERY), (EVERY, EVERY))]

    return [(which, place)]


def squares_kernel(*refs):
    xs, out_ref = refs[:-1], refs[-1]

    @pl.loop(0, out_ref.shape[0] // 64)
    def _(m):
        at = pl.ds(aligned(m * 64, 64), 64)
        total = jnp.zeros((64, 128), F32)
        for block in xs:
            for k in range(0, block.shape[1], 128):
                part = block[at, k : k + 128].astype(F32)
                total += part * part
        out_ref[at, :] = total


def squares(xs):
    rows, tile = xs[0].shape[0], 256
    return pl.pallas_call(
        squares_kernel,
        grid=(rows // tile,),
        out_shape=jax.ShapeDtypeStruct((rows, 128), F32),
        in_specs=[pl.BlockSpec((tile, v.shape[1]), lambda i: (i, 0)) for v in xs],
        out_specs=pl.BlockSpec((tile, 128), lambda i: (i, 0)),
        cost_estimate=cheap(),
    )(*[pltpu.with_memory_space_constraint(v, pltpu.MemorySpace.HBM) for v in xs])


def body(
    reference_rows,
    critic_rows,
    segment_ids,
    pack_dest,
    ref_query,
    ref_key,
    ref_value,
    critic_query,
    critic_key,
    critic_value,
    ref_readout,
    critic_readout,
):
    del pack_dest
    tp = lax.axis_index("tp")
    pos = jnp.stack([tp // 2, tp % 2]).astype(jnp.int32)
    seg_row = segment_ids.reshape(1, -1)
    slots = segment_ids.shape[0]
    half = slots // 2

    ref_w = jnp.concatenate([ref_query, ref_key, ref_value], axis=1)
    gathered = lax.all_gather(ref_w, "rep", axis=0, tiled=True)
    critic_before, critic_after = step_one(critic_rows)
    critic_other, ref_other = swap_core(critic_rows), swap_core(reference_rows)

    critic_before, critic_after, critic_other, ref_rows, ref_other = lax.optimization_barrier(
        (critic_before, critic_after, critic_other, reference_rows, ref_other)
    )
    critic_far = step_two(critic_before, critic_after)
    critic_far, ref_rows = lax.optimization_barrier((critic_far, ref_rows))
    ref_before, ref_after = step_one(ref_rows)
    critic_x = [critic_rows, critic_other]
    for v in (critic_after, critic_before, *critic_far):
        critic_x += [v, swap_core(v)]
    plan_x = [[], [], [], []]
    order = ((0, (0, slots)), (1, (0, slots)), (3, (0, slots)), (2, (0, half)), (2, (half, half)))
    for index, (slot, rows) in enumerate(order):
        for other in range(2):
            plan_x[slot] += critic_rows_plan(2 * index + other, other == 1, rows)
    critic_part = project(
        pos,
        critic_x,
        [critic_query, critic_key, critic_value],
        plan_x,
        [critic_weights(k) for k in range(NX)],
        1024,
        slots,
        finish=(1, 4096, seg_row, critic_readout, None),
    )

    ref_before, ref_after, critic_part = lax.optimization_barrier(
        (ref_before, ref_after, critic_part)
    )
    far = step_two(ref_before, ref_after)
    ref_x = [ref_rows, ref_other]
    for v in (ref_after, ref_before):
        ref_x += [v, swap_core(v)]
    total = squares(ref_x)
    plan_x = [[], [], []]
    for index, slot in enumerate(range(3)):
        for other in range(2):
            plan_x[slot] += ref_rows_plan(2 * index + other, other == 1, (0, slots))
    near = project(
        pos,
        ref_x,
        [gathered],
        plan_x,
        [gathered_weights(0, k) for k in (0, 1, 3)],
        2048,
        slots,
    )
    far, total = lax.optimization_barrier((far, total))
    far_x, plan_x = [], [[]]
    for index, v in enumerate(far):
        far_x += [v, swap_core(v)]
        for other in range(2):
            plan_x[0] += ref_rows_plan(2 * index + other, other == 1, (index * half, half))
    partial = project(
        pos,
        far_x,
        [gathered],
        plan_x,
        [gathered_weights(0, 2)],
        2048,
        slots,
        prior=(total, near),
        finish=(0, 8192, seg_row, ref_readout, critic_part),
    )
    scores = over_tp(partial)
    scores = jnp.where(seg_row >= 0, scores, 0.0)
    return scores[0], scores[1]


def solution(mesh):
    return jax.shard_map(
        body,
        mesh=mesh,
        in_specs=(
            P("rep", "tp"),
            P("rep", "tp"),
            P("rep"),
            P("rep", None),
            P("rep", "tp"),
            P("rep", "tp"),
            P("rep", "tp"),
            P(None, "tp"),
            P(None, "tp"),
            P(None, "tp"),
            P("tp"),
            P("tp"),
        ),
        out_specs=(P("rep"), P("rep")),
        check_vma=False,
    )
```

```python
import functools

import jax
import jax.numpy as jnp
from jax import lax
from jax.experimental import pallas as pl
from jax.experimental.pallas import tpu as pltpu
from jax.sharding import PartitionSpec as P

HD = 128
NX = 4
WIDE = 768
EPS = 1e-05
BF = jnp.bfloat16
F32 = jnp.float32
EVERY = slice(None)


def shift_x(v, k):
    pairs = [(2 * x + c, 2 * ((x + k) % NX) + c) for x in range(NX) for c in range(2)]
    return lax.ppermute(v, "tp", pairs)


def swap_core(v):
    return lax.ppermute(v, "tp", [(t, t ^ 1) for t in range(2 * NX)])


def over_tp(v):
    v = v + swap_core(v)
    return v + shift_x(v, 1) + (shift_x(v, 2) + shift_x(v, 3))


def step_one(v):
    return shift_x(v, 1), shift_x(v, -1)


def step_two(before, after):
    half = before.shape[0] // 2
    return shift_x(before[:half], 1), shift_x(after[half:], -1)


def aligned(value, step):
    return pl.multiple_of(value, step)


def cheap():
    return pl.CostEstimate(flops=1024, bytes_accessed=1024, transcendentals=0)


def attend_tiles(acc, squares, depth, seg_ref, read_ref, more_ref, out_ref):
    tile = 128
    jds = lax.broadcasted_iota(jnp.int32, (tile, tile), 0)
    ids = lax.broadcasted_iota(jnp.int32, (tile, tile), 1)

    @pl.loop(0, acc.shape[0] // tile // 4)
    def _(four):
        for u in range(4):
            at = pl.ds(aligned((four * 4 + u) * tile, tile), tile)
            part = acc[at, :].astype(BF)
            queries = jnp.concatenate([part[:, h * HD : (h + 1) * HD] for h in range(4)], axis=0)
            keys, values = part[:, 4 * HD : 5 * HD], part[:, 5 * HD :]
            segs = jnp.broadcast_to(seg_ref[:, at], (tile, tile))
            allowed = (jds <= ids) & (segs.T == segs)
            mean = jnp.sum(squares[at, :], axis=-1, keepdims=True) * (1.0 / depth)
            key_scale = jnp.broadcast_to(lax.rsqrt(mean + EPS), (tile, tile))
            both = key_scale * key_scale.T * HD ** (-0.5)
            scores = lax.dot_general(
                keys, queries, (((1,), (1,)), ((), ())), preferred_element_type=F32
            )
            hidden = jnp.concatenate([jnp.where(allowed, 0.0, -1e30)] * 4, axis=1) < 0.0
            masked = jnp.where(hidden, -1e30, scores * jnp.concatenate([both] * 4, axis=1))
            powers = jnp.exp(masked - jnp.max(masked, axis=0, keepdims=True))
            inverse = 1.0 / jnp.sum(powers, axis=0, keepdims=True)
            weights = (powers * inverse * jnp.concatenate([key_scale] * 4, axis=1)).astype(BF)
            mixture = lax.dot_general(
                values, weights, (((0,), (0,)), ((), ())), preferred_element_type=F32
            ).astype(BF)
            total = jnp.zeros((8, tile), F32)
            for h in range(4):
                total += jnp.dot(
                    read_ref[h], mixture[:, h * tile : (h + 1) * tile], preferred_element_type=F32
                )
            if more_ref is not None:
                total += more_ref[:, at]
            out_ref[:, at] = total


def start_copies(pos, src, dst, sem, place):
    condition, copies = place(pos)

    def start():
        for from_, to in copies:
            pltpu.make_async_copy(src.at[from_], dst.at[to], sem).start()

    if condition is None:
        start()
    else:
        pl.when(condition)(start)


def project_kernel(plan_x, plan_w, n_x, n_w, prior, finish, *refs):
    pos, refs = refs[0], refs[1:]
    xs, ws, refs = refs[:n_x], refs[n_x : n_x + n_w], refs[n_x + n_w :]
    if prior:
        prior_squares, refs = refs[0], refs[1:]
    prior_ref, refs = (refs[0], refs[1:]) if prior > 1 else (None, refs)
    if finish:
        seg_ref, read_ref, refs = refs[0], refs[1], refs[2:]
        more_ref, refs = (refs[0], refs[1:]) if finish[1] else (None, refs)
        out_ref, xbuf, wbuf, sems, acc, squares = refs
    else:
        acc, xbuf, wbuf, sems = refs
        squares = None
    slots, rows, width = xbuf.shape
    for slot in range(slots):
        for plan, sources, dst, kind in ((plan_x, xs, xbuf, 0), (plan_w, ws, wbuf, 1)):
            for which, place in plan[slot]:
                start_copies(pos, sources[which], dst.at[slot], sems.at[kind, slot], place)
    acc[...] = prior_ref[...] if prior > 1 else jnp.zeros(acc.shape, F32)
    if finish:
        squares[...] = prior_squares[...] if prior else jnp.zeros(squares.shape, F32)

    @pl.loop(0, slots)
    def _(s):
        pltpu.make_async_copy(xbuf.at[s], xbuf.at[s], sems.at[0, s]).wait()

        if finish:

            @pl.loop(0, rows // 64)
            def _(m):
                at = pl.ds(aligned(m * 64, 64), 64)
                total = squares[at, :]
                for k in range(0, width, 128):
                    part = xbuf[s, at, k : k + 128].astype(F32)
                    total += part * part
                squares[at, :] = total

        pltpu.make_async_copy(wbuf.at[s], wbuf.at[s], sems.at[1, s]).wait()

        @pl.loop(0, rows // 1024)
        def _(m):
            at = pl.ds(aligned(m * 1024, 1024), 1024)
            for k in range(0, width, 1024):
                acc[at, :] += jnp.dot(
                    xbuf[s, at, k : k + 1024], wbuf[s, k : k + 1024, :], preferred_element_type=F32
                )

    if finish:
        attend_tiles(acc, squares, finish[0], seg_ref, read_ref, more_ref, out_ref)


def project(pos, xs, ws, plan_x, plan_w, width, rows, prior=(), finish=None):
    slots = len(plan_x)
    vmem = pl.BlockSpec(memory_space=pltpu.VMEM)
    operands = [pos] + [
        pltpu.with_memory_space_constraint(v, pltpu.MemorySpace.HBM) for v in (*xs, *ws)
    ]
    specs = [pl.BlockSpec(memory_space=pltpu.SMEM)]
    specs += [pl.BlockSpec(memory_space=pltpu.MemorySpace.HBM)] * (len(xs) + len(ws))
    operands += prior
    specs += [vmem] * len(prior)
    scratch = [
        pltpu.VMEM((slots, rows, width), BF),
        pltpu.VMEM((slots, width, WIDE), BF),
        pltpu.SemaphoreType.DMA((2, slots)),
    ]
    out = jax.ShapeDtypeStruct((rows, WIDE), F32)
    static = None
    if finish:
        index, depth, segments, readout, more = finish
        at_row = (jnp.arange(8) == index)[None, :, None]
        read = jnp.where(at_row, readout.reshape(4, 1, HD), jnp.zeros((), BF))
        extra = [segments, read] + ([more] if more is not None else [])
        operands += extra
        specs += [vmem] * len(extra)
        scratch += [pltpu.VMEM((rows, WIDE), F32), pltpu.VMEM((rows, 128), F32)]
        out = jax.ShapeDtypeStruct((8, rows), F32)
        static = (depth, more is not None)
    return pl.pallas_call(
        functools.partial(
            project_kernel, plan_x, plan_w, len(xs), len(ws), len(prior), static
        ),
        out_shape=out,
        in_specs=specs,
        out_specs=vmem,
        scratch_shapes=scratch,
        compiler_params=pltpu.CompilerParams(vmem_limit_bytes=48 * 1024 * 1024),
        cost_estimate=cheap(),
    )(*operands)


def origin(pos, ahead):
    return lax.rem(pos[0] + ahead, NX)


def side(pos, other):
    return 1 - pos[1] if other else pos[1]


def critic_rows_plan(which, other, rows):
    def place(pos):
        to = (pl.ds(*rows), pl.ds(aligned(side(pos, other) * 512, 512), 512))
        return None, [((EVERY, EVERY), to)]

    return [(which, place)]


def critic_weights(ahead):
    plan = []
    for which, (lane, size) in enumerate(((0, 512), (512, 128), (640, 128))):

        def place(pos, lane=lane, size=size):
            rows = pl.ds(aligned(origin(pos, ahead) * 1024, 1024), 1024)
            return None, [((rows, EVERY), (EVERY, pl.ds(lane, size)))]

        plan.append((which, place))
    return plan


def ref_rows_plan(which, other, rows):
    def place(pos):
        to = (pl.ds(*rows), pl.ds(aligned(side(pos, other) * 1024, 1024), 1024))
        return None, [((EVERY, EVERY), to)]

    return [(which, place)]


def gathered_weights(which, ahead):
    def place(pos):
        rows = pl.ds(aligned(origin(pos, ahead) * 2048, 2048), 2048)
        return None, [((rows, EVERY), (EVERY, EVERY))]

    return [(which, place)]


def whole_plan(which, rows):
    return [(which, lambda pos: (None, [((EVERY, EVERY), (pl.ds(*rows), EVERY))]))]


def side_weights(which, ahead, other):
    def place(pos):
        first = origin(pos, ahead) * 2048 + side(pos, other) * 1024
        return None, [((pl.ds(aligned(first, 1024), 1024), EVERY), (EVERY, EVERY))]

    return [(which, place)]


def squares_kernel(*refs):
    xs, out_ref = refs[:-1], refs[-1]

    @pl.loop(0, out_ref.shape[0] // 64)
    def _(m):
        at = pl.ds(aligned(m * 64, 64), 64)
        total = jnp.zeros((64, 128), F32)
        for block in xs:
            for k in range(0, block.shape[1], 128):
                part = block[at, k : k + 128].astype(F32)
                total += part * part
        out_ref[at, :] = total


def squares(xs):
    rows, tile = xs[0].shape[0], 256
    return pl.pallas_call(
        squares_kernel,
        grid=(rows // tile,),
        out_shape=jax.ShapeDtypeStruct((rows, 128), F32),
        in_specs=[pl.BlockSpec((tile, v.shape[1]), lambda i: (i, 0)) for v in xs],
        out_specs=pl.BlockSpec((tile, 128), lambda i: (i, 0)),
        cost_estimate=cheap(),
    )(*[pltpu.with_memory_space_constraint(v, pltpu.MemorySpace.HBM) for v in xs])


def body(
    reference_rows,
    critic_rows,
    segment_ids,
    pack_dest,
    ref_query,
    ref_key,
    ref_value,
    critic_query,
    critic_key,
    critic_value,
    ref_readout,
    critic_readout,
):
    del pack_dest
    tp = lax.axis_index("tp")
    pos = jnp.stack([tp // 2, tp % 2]).astype(jnp.int32)
    seg_row = segment_ids.reshape(1, -1)
    slots = segment_ids.shape[0]
    half = slots // 2

    ref_w = jnp.concatenate([ref_query, ref_key, ref_value], axis=1)
    gathered = lax.all_gather(ref_w, "rep", axis=0, tiled=True)
    critic_before, critic_after = step_one(critic_rows)
    critic_other, ref_other = swap_core(critic_rows), swap_core(reference_rows)

    critic_before, critic_after, critic_other, ref_rows, ref_other = lax.optimization_barrier(
        (critic_before, critic_after, critic_other, reference_rows, ref_other)
    )
    critic_far = step_two(critic_before, critic_after)
    critic_far, ref_rows = lax.optimization_barrier((critic_far, ref_rows))
    ref_before, ref_after = step_one(ref_rows)
    critic_x = [critic_rows, critic_other]
    for v in (critic_after, critic_before, *critic_far):
        critic_x += [v, swap_core(v)]
    plan_x = [[], [], [], []]
    order = ((0, (0, slots)), (1, (0, slots)), (3, (0, slots)), (2, (0, half)), (2, (half, half)))
    for index, (slot, rows) in enumerate(order):
        for other in range(2):
            plan_x[slot] += critic_rows_plan(2 * index + other, other == 1, rows)
    critic_part = project(
        pos,
        critic_x,
        [critic_query, critic_key, critic_value],
        plan_x,
        [critic_weights(k) for k in range(NX)],
        1024,
        slots,
        finish=(1, 4096, seg_row, critic_readout, None),
    )

    ref_before, ref_after, critic_part = lax.optimization_barrier(
        (ref_before, ref_after, critic_part)
    )
    far = step_two(ref_before, ref_after)
    ref_x = [ref_rows, ref_other]
    for v in (ref_after, ref_before):
        ref_x += [v, swap_core(v)]
    total = squares(ref_x)
    plan_x = [[], [], []]
    for index, slot in enumerate(range(3)):
        for other in range(2):
            plan_x[slot] += ref_rows_plan(2 * index + other, other == 1, (0, slots))
    near = project(
        pos,
        ref_x,
        [gathered],
        plan_x,
        [gathered_weights(0, k) for k in (0, 1, 3)],
        2048,
        slots,
    )
    far, total = lax.optimization_barrier((far, total))
    far_x, plan_x = [], [[], []]
    for index, v in enumerate(far):
        far_x += [v, swap_core(v)]
        for other in range(2):
            plan_x[other] += whole_plan(2 * index + other, (index * half, half))
    partial = project(
        pos,
        far_x,
        [gathered],
        plan_x,
        [side_weights(0, 2, other == 1) for other in range(2)],
        1024,
        slots,
        prior=(total, near),
        finish=(0, 8192, seg_row, ref_readout, critic_part),
    )
    scores = over_tp(partial)
    scores = jnp.where(seg_row >= 0, scores, 0.0)
    return scores[0], scores[1]


def solution(mesh):
    return jax.shard_map(
        body,
        mesh=mesh,
        in_specs=(
            P("rep", "tp"),
            P("rep", "tp"),
            P("rep"),
            P("rep", None),
            P("rep", "tp"),
            P("rep", "tp"),
            P("rep", "tp"),
            P(None, "tp"),
            P(None, "tp"),
            P(None, "tp"),
            P("tp"),
            P("tp"),
        ),
        out_specs=(P("rep"), P("rep")),
        check_vma=False,
    )
```
